32 devices in a mesh: groups: 2 (over x), rows: 16 (over z, y, core).
Axes of the slice: x: 2, y: 2, z: 4, core: 2. Of those that a mesh axis runs over, the one named last changes fastest.
Arguments:
- bin_ids: int32 [16384, 512], P(('groups', 'rows')), parts along dimension 0, may hold values from 0 to 255
- gradients: bfloat16 [16384], P(('groups', 'rows')), parts along dimension 0, may hold values from -6 to 6
- hessians: bfloat16 [16384], P(('groups', 'rows')), parts along dimension 0, may hold values from 0.049804688 to 1
- node_ids: int32 [16384], P(('groups', 'rows')), parts along dimension 0, may hold values from 0 to 15
- predictions: float32 [16384], P(('groups', 'rows')), parts along dimension 0, may hold values from -6 to 6
- split_feature: int32 [32], P('groups'), parts along dimension 0, may hold values from 0 to 511
- split_bin: int32 [32], P('groups'), parts along dimension 0, may hold values from 0 to 254
Outputs:
- gains: float32 [1024, 16, 256], P(('groups', 'rows')), parts along dimension 0
- best_gain: float32 [32], P('groups'), parts along dimension 0
- leaf_values: float32 [2, 32], P(None, 'groups'), parts along dimension 1
- new_predictions: float32 [16384], P(('groups', 'rows')), parts along dimension 0
The draws below stay inside these ranges and needn't reach their ends.
There are 2 independent parts, one for each index of `groups`. The reference program is written for one: setup_inputs(seed, part) draws one part's arguments, and reference() takes and returns one part's arrays. A program takes and returns all parts, laid end to end along the dimension named above; each array names one. Nothing has to cross between parts.
All inputs are finite; a program needn't handle non-finite values.
Results may differ from the reference program's by a relative error of at most 0.0003.
Values sent between devices are 32-bit elements; how exact they have to be, the bound alone decides.
A program may use at most 64 MiB of HBM per device.

```python
import math
import jax
import jax.numpy as jnp
import numpy as np

F = 512
BINS = 256
NODES = 16
ROWS = 8192


def with_ends(result, own_key, least, high):
    index_at = [jax.random.randint(jax.random.fold_in(own_key, axis), (), 0, length) for axis, length in enumerate(result.shape)]
    widest = result.shape.index(max(result.shape))
    neighbour = index_at[:widest] + [(index_at[widest] + 1) % result.shape[widest]] + index_at[widest + 1:]
    return result.at[tuple(index_at)].set(least).at[tuple(neighbour)].set(high)


def block_levels(stream_key, extent, pieces, smallest, largest):
    def one(dim, parts):
        heights = jax.random.uniform(jax.random.fold_in(jax.random.fold_in(stream_key, 6), dim), (parts,), jnp.float32, smallest / len(pieces), largest / len(pieces))
        return jnp.repeat(jnp.exp(heights), extent[dim] // parts).reshape((-1,) + (1,) * (len(extent) - dim - 1))

    loudness = one(*pieces[0])
    for cut in pieces[1:]:
        loudness = loudness * one(*cut)
    return loudness


def rank_table(amount, skew):
    weights = [(1 << 20) // math.isqrt(standing ** skew) + 1 for standing in range(1, amount + 1)]
    deviation = 1 + sum(weights) // (1 << 30)
    return np.cumsum(np.array([max(1, weight // deviation) for weight in weights]))


def skewed_ids(key, shape, amount, slope):
    grid = rank_table(amount, slope)
    ticket = jax.random.randint(jax.random.fold_in(key, 1), shape, 0, int(grid[amount - 1]))
    rank = jnp.searchsorted(jnp.asarray(grid, jnp.int32), ticket, side="right")
    return jax.random.permutation(jax.random.fold_in(key, 2), amount)[rank].astype(jnp.int32)


def gaussian(key, extent, scale, most, pieces=(), kind=jnp.bfloat16):
    result = jax.random.normal(key, extent, jnp.float32) * scale
    if len(pieces) > 0:
        result = block_levels(key, extent, pieces, -0.22, 0.18) * result
    return jnp.clip(result, min=-most, max=most).astype(kind)


def setup_inputs(seed: int = 0, part: int = 0) -> dict:
    splits = jax.random.split(jax.random.key(seed), 8)
    part_splits = jax.random.split(jax.random.fold_in(splits[7], part), 8)
    bin_ids = with_ends(jax.random.randint(part_splits[0], (ROWS, F), 0, BINS), jax.random.fold_in(part_splits[0], 1), 0, BINS - 1).astype(jnp.int32)
    gradients = gaussian(part_splits[1], (ROWS,), 1.0, 6.0, ((0, 16),))
    hessians = jnp.clip(jnp.exp(math.log(1.0) - 2.9996462 * jax.random.uniform(part_splits[2], (ROWS,), jnp.float32) ** block_levels(part_splits[2], (ROWS,), ((0, 16),), -0.2, 0.2)), 0.049804688, 1.0).astype(jnp.bfloat16)
    node_ids = with_ends(skewed_ids(part_splits[3], (ROWS,), NODES, 2), jax.random.fold_in(part_splits[3], 3), 0, NODES - 1).astype(jnp.int32)
    predictions = gaussian(part_splits[4], (ROWS,), 1.0, 6.0, ((0, 16),), jnp.float32)
    split_feature = with_ends(jax.random.randint(part_splits[5], (NODES,), 0, F), jax.random.fold_in(part_splits[5], 1), 0, F - 1).astype(jnp.int32)
    split_bin = with_ends(jax.random.randint(part_splits[6], (NODES,), 0, BINS - 1), jax.random.fold_in(part_splits[6], 1), 0, (BINS - 1) - 1).astype(jnp.int32)
    return {"bin_ids": bin_ids, "gradients": gradients, "hessians": hessians, "node_ids": node_ids, "predictions": predictions, "split_feature": split_feature, "split_bin": split_bin}


l2_penalty = 1.0
shrinkage = 0.5


def histogram_of(values, slot_ids, shape_like):
    spread = jnp.broadcast_to(values.astype(jnp.float32)[:, None], shape_like).reshape(-1)
    summed = jax.ops.segment_sum(spread, slot_ids, num_segments=NODES * F * BINS)
    return summed.reshape(NODES, F, BINS).transpose(1, 0, 2)


def reference(bin_ids, gradients, hessians, node_ids, predictions, split_feature, split_bin):
    feature_base = jnp.arange(F, dtype=jnp.int32) * BINS
    slot_ids = (node_ids[:, None] * (F * BINS) + feature_base[None, :] + bin_ids).astype(jnp.int32).reshape(-1)
    hist_grad = histogram_of(gradients, slot_ids, bin_ids.shape)
    hist_hess = histogram_of(hessians, slot_ids, bin_ids.shape)
    cum_grad = jnp.cumsum(hist_grad, axis=2)
    cum_hess = jnp.cumsum(hist_hess, axis=2)
    tot_grad = cum_grad[:, :, -1:]
    tot_hess = cum_hess[:, :, -1:]
    gains = 0.5 * (cum_grad ** 2 / (cum_hess + l2_penalty)
                   + (tot_grad - cum_grad) ** 2 / (tot_hess - cum_hess + l2_penalty)
                   - tot_grad ** 2 / (tot_hess + l2_penalty))
    best_gain = jnp.max(gains, axis=(0, 2))
    node_range = jnp.arange(NODES, dtype=jnp.int32)
    left_grad = cum_grad[split_feature, node_range, split_bin]
    left_hess = cum_hess[split_feature, node_range, split_bin]
    node_grad = tot_grad[split_feature, node_range, 0]
    node_hess = tot_hess[split_feature, node_range, 0]
    leaf_left = -left_grad / (left_hess + l2_penalty)
    leaf_right = -(node_grad - left_grad) / (node_hess - left_hess + l2_penalty)
    leaf_values = jnp.stack([leaf_left, leaf_right])
    row_feature = split_feature[node_ids]
    row_bin = jnp.take_along_axis(bin_ids, row_feature[:, None], axis=1)[:, 0]
    go_right = row_bin > split_bin[node_ids]
    new_predictions = predictions + shrinkage * jnp.where(go_right, leaf_right[node_ids], leaf_left[node_ids])
    return gains, best_gain, leaf_values, new_predictions
```

```python
import functools

import jax
import jax.numpy as jnp
from jax import lax
from jax.experimental import pallas as pl
from jax.experimental.pallas import tpu as pltpu
from jax.sharding import PartitionSpec as P

BINS = 256
NODES = 16
LANES = 128
HALVES = BINS // LANES

l2_penalty = 1.0
shrinkage = 0.5

f32 = jnp.float32
bf16 = jnp.bfloat16


def flipped(me, step, n):
    if n & (n - 1):
        return (step + n - me) % n
    out, bit = 0, 1
    while bit < n:
        out = out + (((me // bit) % 2 + (step // bit) % 2) % 2) * bit
        bit *= 2
    return out


def to_row(column):
    shape = (column.shape[0], LANES)
    diagonal = lax.broadcasted_iota(jnp.int32, shape, 0) == lax.broadcasted_iota(
        jnp.int32, shape, 1
    )
    return jnp.sum(jnp.where(diagonal, column, 0.0), axis=0, keepdims=True)


def kernel(
    n,
    bins_ref,
    rows_ref,
    split_ref,
    gains_ref,
    best_ref,
    leaf_ref,
    pred_ref,
    send_bins,
    send_meta,
    recv_bins,
    recv_meta,
    send_best,
    recv_best,
    acc,
    bins_out,
    bins_in,
    meta_out,
    meta_in,
    best_out,
    best_in,
):
    owned = recv_bins.shape[1]
    local = recv_bins.shape[2]
    features = owned * n
    me = lax.axis_index("rows")

    barrier = pltpu.get_barrier_semaphore()

    def greet(step, carry):
        pl.semaphore_signal(
            barrier, inc=1, device_id={"rows": flipped(me, step, n)},
            device_id_type=pl.DeviceIdType.MESH,
        )
        return carry

    def all_steps(body):
        lax.fori_loop(1, n, body, 0)

    all_steps(greet)

    width = min(features, LANES)
    chosen = split_ref[:, 0:1]
    node_bin = jnp.zeros((NODES, local), f32)
    for tile in range(features // width):
        turned = jnp.transpose(bins_ref[:, tile * width : (tile + 1) * width].astype(f32))
        for j in range(width // owned):
            send_bins[tile * (width // owned) + j] = turned[j * owned : (j + 1) * owned]
        feature = lax.broadcasted_iota(jnp.int32, (NODES, width), 1) + tile * width
        pick = jnp.where(feature == chosen, 1.0, 0.0).astype(bf16)
        node_bin = node_bin + jnp.dot(
            pick, turned.astype(bf16), preferred_element_type=f32
        )

    node = lax.broadcasted_iota(jnp.int32, (NODES, local), 0).astype(f32)
    node_hot = node == rows_ref[2:3]
    beyond = node_bin > split_ref[:, 1:2].astype(f32)
    side = jnp.sum(jnp.where(node_hot & beyond, 1.0, 0.0), axis=0, keepdims=True)
    send_meta[0:3] = rows_ref[0:3]
    send_meta[3:4] = side
    recv_bins[me] = send_bins[me]
    recv_meta[me] = send_meta[...]

    pl.semaphore_wait(barrier, n - 1)

    def bins_copy(step):
        to = flipped(me, step, n)
        return pltpu.make_async_remote_copy(
            src_ref=send_bins.at[to], dst_ref=recv_bins.at[me],
            send_sem=bins_out.at[to], recv_sem=bins_in.at[me],
            device_id={"rows": to}, device_id_type=pl.DeviceIdType.MESH,
        )

    def meta_copy(step):
        to = flipped(me, step, n)
        return pltpu.make_async_remote_copy(
            src_ref=send_meta, dst_ref=recv_meta.at[me],
            send_sem=meta_out.at[to], recv_sem=meta_in.at[me],
            device_id={"rows": to}, device_id_type=pl.DeviceIdType.MESH,
        )

    def best_copy(step):
        to = flipped(me, step, n)
        return pltpu.make_async_remote_copy(
            src_ref=send_best, dst_ref=recv_best.at[me],
            send_sem=best_out.at[to], recv_sem=best_in.at[me],
            device_id={"rows": to}, device_id_type=pl.DeviceIdType.MESH,
        )

    def landed(buffer, sems, source):
        pltpu.make_async_copy(buffer.at[source], buffer.at[source], sems.at[source]).wait()

    def start(step, carry):
        meta_copy(step).start()
        bins_copy(step).start()
        return carry

    all_steps(start)

    acc[...] = jnp.zeros_like(acc)
    low = lax.broadcasted_iota(jnp.int32, (LANES, LANES), 0).astype(bf16)
    low = jnp.concatenate([low] * (local // LANES), axis=1)
    one = jnp.ones((), bf16)
    zero = jnp.zeros((), bf16)
    group = 4 if owned % 4 == 0 else 1

    def accumulate(step, sums):
        left_sum, node_sum = sums
        source = flipped(me, step, n)

        @pl.when(step > 0)
        def _():
            landed(recv_meta, meta_in, source)
            landed(recv_bins, bins_in, source)

        meta = recv_meta[source]
        hot = node == meta[2:3]
        exact = jnp.concatenate(
            [jnp.where(hot, meta[0:1], 0.0), jnp.where(hot, meta[1:2], 0.0)], axis=0
        )
        left = jnp.where(meta[3:4] == 0.0, exact, 0.0)
        for tile in range(local // LANES):
            lanes = slice(tile * LANES, (tile + 1) * LANES)
            left_sum = left_sum + left[:, lanes]
            node_sum = node_sum + exact[:, lanes]
        weights = exact.astype(bf16)

        def some_features(block, carry):
            for j in range(group):
                f = block * group + j
                row = recv_bins[source, pl.ds(f, 1), :]
                high = jnp.floor(row * (1.0 / LANES))
                rest = (row - high * LANES).astype(bf16)
                high = jnp.broadcast_to(high.astype(bf16), weights.shape)
                upto = jnp.where(rest <= low, one, zero)
                parts = [weights] + [
                    jnp.where(high == float(h), weights, zero) for h in range(1, HALVES)
                ]
                acc[f] += lax.dot_general(
                    jnp.concatenate(parts, axis=0), upto, (((1,), (1,)), ((), ())),
                    preferred_element_type=f32,
                )
            return carry

        lax.fori_loop(0, owned // group, some_features, 0)
        return left_sum, node_sum

    blank = jnp.zeros((2 * NODES, LANES), f32)
    left_sum, node_sum = lax.fori_loop(0, n, accumulate, (blank, blank))

    def score(f, best):
        table = acc[f]
        upper = [table[2 * NODES * h : 2 * NODES * (h + 1)] for h in range(1, HALVES)]
        first = table[0 : 2 * NODES]
        for part in upper:
            first = first - part
        offset = jnp.zeros((2 * NODES, 1), f32)
        sums = []
        for part in [first] + upper:
            sums.append(part + offset)
            offset = offset + part[:, LANES - 1 : LANES]
        tot_grad, tot_hess = offset[:NODES], offset[NODES:]
        whole = tot_grad * tot_grad / (tot_hess + l2_penalty)
        for h, part in enumerate(sums):
            cum_grad, cum_hess = part[:NODES], part[NODES:]
            rest_grad = tot_grad - cum_grad
            gain = 0.5 * (
                cum_grad * cum_grad / (cum_hess + l2_penalty)
                + rest_grad * rest_grad / (tot_hess - cum_hess + l2_penalty)
                - whole
            )
            gains_ref[f, :, h * LANES : (h + 1) * LANES] = gain
            best = jnp.maximum(best, gain)
        return best

    best = lax.fori_loop(0, owned, score, jnp.full((NODES, LANES), -jnp.inf, f32))
    send_best[...] = to_row(jnp.max(best, axis=1, keepdims=True))
    recv_best[me] = send_best[...]

    def start_best(step, carry):
        best_copy(step).start()
        return carry

    all_steps(start_best)

    left_sum = jnp.sum(left_sum, axis=1, keepdims=True)
    node_sum = jnp.sum(node_sum, axis=1, keepdims=True)
    left_grad, left_hess = left_sum[:NODES], left_sum[NODES:]
    right_grad = node_sum[:NODES] - left_grad
    right_hess = node_sum[NODES:] - left_hess
    leaf_left = -left_grad / (left_hess + l2_penalty)
    leaf_right = -right_grad / (right_hess + l2_penalty)
    leaf_ref[0:1] = to_row(leaf_left)
    leaf_ref[1:2] = to_row(leaf_right)
    value = jnp.where(beyond, leaf_right, leaf_left)
    moved = jnp.sum(jnp.where(node_hot, value, 0.0), axis=0, keepdims=True)
    pred_ref[...] = rows_ref[3:4] + shrinkage * moved

    def finish(step, carry):
        meta_copy(step).wait_send()
        bins_copy(step).wait_send()
        best_copy(step).wait_send()
        landed(recv_best, best_in, flipped(me, step, n))
        return carry

    all_steps(finish)
    best_ref[...] = jnp.max(recv_best[...], axis=0)


def body(n, bin_ids, gradients, hessians, node_ids, predictions, split_feature, split_bin):
    local, features = bin_ids.shape
    owned = features // n
    rows = jnp.stack(
        [gradients.astype(f32), hessians.astype(f32), node_ids.astype(f32), predictions]
    )
    splits = jnp.stack([split_feature, split_bin], axis=1)
    vmem = pl.BlockSpec(memory_space=pltpu.VMEM)
    gains, best, leaf, pred = pl.pallas_call(
        functools.partial(kernel, n),
        out_shape=(
            jax.ShapeDtypeStruct((owned, NODES, BINS), f32),
            jax.ShapeDtypeStruct((1, LANES), f32),
            jax.ShapeDtypeStruct((2, LANES), f32),
            jax.ShapeDtypeStruct((1, local), f32),
        ),
        in_specs=[vmem] * 3,
        out_specs=(vmem,) * 4,
        scratch_shapes=[
            pltpu.VMEM((n, owned, local), f32),
            pltpu.VMEM((4, local), f32),
            pltpu.VMEM((n, owned, local), f32),
            pltpu.VMEM((n, 4, local), f32),
            pltpu.VMEM((1, LANES), f32),
            pltpu.VMEM((n, 1, LANES), f32),
            pltpu.VMEM((owned, 2 * NODES * HALVES, LANES), f32),
        ]
        + [pltpu.SemaphoreType.DMA((n,))] * 6,
        compiler_params=pltpu.CompilerParams(
            collective_id=0, has_side_effects=True, vmem_limit_bytes=48 << 20
        ),
        name="split_finding",
    )(bin_ids, rows, splits)
    return gains, best[0, :NODES], leaf[:, :NODES], pred[0]


def solution(mesh):
    both = P(("groups", "rows"))
    return jax.shard_map(
        functools.partial(body, mesh.shape["rows"]),
        mesh=mesh,
        in_specs=(
            P(("groups", "rows"), None), both, both, both, both, P("groups"), P("groups"),
        ),
        out_specs=(P(("groups", "rows"), None, None), P("groups"), P(None, "groups"), both),
        check_vma=False,
    )
```

```python
import functools
import math

import jax
import jax.numpy as jnp
from jax import lax
from jax.experimental import pallas as pl
from jax.experimental.pallas import tpu as pltpu
from jax.sharding import PartitionSpec as P

BINS = 256
NODES = 16
LANES = 128
HALVES = BINS // LANES

l2_penalty = 1.0
shrinkage = 0.5

f32 = jnp.float32
bf16 = jnp.bfloat16


def flipped(me, step, n):
    out, bit = 0, 1
    while bit < n:
        out = out + (((me // bit) % 2 + (step // bit) % 2) % 2) * bit
        bit *= 2
    return out


def to_row(column):
    shape = (column.shape[0], LANES)
    diagonal = lax.broadcasted_iota(jnp.int32, shape, 0) == lax.broadcasted_iota(
        jnp.int32, shape, 1
    )
    return jnp.sum(jnp.where(diagonal, column, 0.0), axis=0, keepdims=True)


def to_column(row):
    shape = (row.shape[1], row.shape[1])
    diagonal = lax.broadcasted_iota(jnp.int32, shape, 0) == lax.broadcasted_iota(
        jnp.int32, shape, 1
    )
    return jnp.sum(jnp.where(diagonal, row, 0.0), axis=1, keepdims=True)


def in_one_row(packed):
    pieces = [packed[j : j + 1].astype(f32) for j in range(packed.shape[0])]
    return jnp.concatenate(pieces, axis=1)


def kernel(
    n,
    bins_hbm,
    grad_hbm,
    hess_hbm,
    node_hbm,
    pred_hbm,
    feature_hbm,
    bin_hbm,
    gains_ref,
    best_ref,
    leaf_ref,
    pred_ref,
    bins_ref,
    grad_ref,
    hess_ref,
    node_ref,
    old_ref,
    feature_ref,
    bin_ref,
    send_bins,
    send_meta,
    recv_bins,
    recv_meta,
    send_stat,
    recv_stat,
    send_best,
    recv_best,
    acc,
    tile_sem,
    small_sem,
    bins_out,
    bins_in,
    meta_out,
    meta_in,
    stat_out,
    stat_in,
    best_out,
    best_in,
):
    owned = recv_bins.shape[1]
    local = recv_bins.shape[2]
    features = owned * n
    me = lax.axis_index("rows")
    width = bins_ref.shape[2]
    tiles = features // width
    per_tile = width // owned

    small = [
        pltpu.make_async_copy(source, target, small_sem.at[i])
        for i, (source, target) in enumerate(
            [
                (grad_hbm, grad_ref),
                (hess_hbm, hess_ref),
                (node_hbm, node_ref),
                (feature_hbm, feature_ref),
                (bin_hbm, bin_ref),
                (pred_hbm, old_ref),
            ]
        )
    ]
    for copy in small:
        copy.start()

    order = list(range(tiles))
    mine = me // per_tile
    tile_at = [flipped(mine, s, tiles) for s in order]
    loads = []
    for i, tile in enumerate(tile_at):
        columns = pl.ds(pl.multiple_of(tile * width, width), width)
        loads.append(
            pltpu.make_async_copy(bins_hbm.at[:, columns], bins_ref.at[i], tile_sem.at[i])
        )
        loads[-1].start()

    barrier = pltpu.get_barrier_semaphore()

    def all_steps(body):
        lax.fori_loop(1, n, body, 0)

    def greet(step, carry):
        pl.semaphore_signal(
            barrier, inc=1, device_id={"rows": flipped(me, step, n)},
            device_id_type=pl.DeviceIdType.MESH,
        )
        return carry

    all_steps(greet)

    def remote(to, source, target, out_sem, in_sem):
        return pltpu.make_async_remote_copy(
            src_ref=source, dst_ref=target.at[me],
            send_sem=out_sem.at[to], recv_sem=in_sem.at[me],
            device_id={"rows": to}, device_id_type=pl.DeviceIdType.MESH,
        )

    def bins_copy(to):
        return remote(to, send_bins.at[to], recv_bins, bins_out, bins_in)

    def meta_copy(to):
        return remote(to, send_meta, recv_meta, meta_out, meta_in)

    def stat_copy(to):
        return remote(to, send_stat, recv_stat, stat_out, stat_in)

    def best_copy(to):
        return remote(to, send_best, recv_best, best_out, best_in)

    def landed(buffer, sems, source):
        pltpu.make_async_copy(buffer.at[source], buffer.at[source], sems.at[source]).wait()

    for copy in small:
        copy.wait()
    send_meta[0:1] = in_one_row(grad_ref[...])
    send_meta[1:2] = in_one_row(hess_ref[...])
    send_meta[2:3] = node_ref[...].astype(f32)
    recv_meta[me] = send_meta[...]
    chosen = to_column(feature_ref[...].astype(f32))
    threshold = to_column(bin_ref[...].astype(f32))
    node = lax.broadcasted_iota(jnp.int32, (NODES, local), 0).astype(f32)
    node_hot = node == send_meta[2:3]

    pl.semaphore_wait(barrier, n - 1)

    def start_meta(step, carry):
        meta_copy(flipped(me, step, n)).start()
        return carry

    def send_tile(tile):
        def start(j, carry):
            to = tile * per_tile + flipped(me % per_tile, j, per_tile)

            @pl.when(to != me)
            def _():
                bins_copy(to).start()

            return carry

        lax.fori_loop(0, per_tile, start, 0)

    node_bin = jnp.zeros((NODES, local), f32)
    for i, tile in enumerate(tile_at):
        loads[i].wait()
        turned = jnp.transpose(bins_ref[i].astype(f32))
        for j in range(per_tile):
            send_bins[tile * per_tile + j] = turned[j * owned : (j + 1) * owned]
        if i == 0:
            all_steps(start_meta)
        else:
            send_tile(tile_at[i - 1])
        feature = lax.broadcasted_iota(jnp.int32, (NODES, width), 1) + tile * width
        pick = jnp.where(feature.astype(f32) == chosen, 1.0, 0.0).astype(bf16)
        node_bin = node_bin + jnp.dot(
            pick, turned.astype(bf16), preferred_element_type=f32
        )
    send_tile(tile_at[-1])
    recv_bins[me] = send_bins[me]

    beyond = node_bin > threshold
    for i, hot in enumerate((node_hot & jnp.logical_not(beyond), node_hot)):
        exact = jnp.concatenate(
            [jnp.where(hot, send_meta[0:1], 0.0), jnp.where(hot, send_meta[1:2], 0.0)], axis=0
        )
        send_stat[i : i + 1] = to_row(jnp.sum(exact, axis=1, keepdims=True))
    recv_stat[me] = send_stat[...]

    acc[...] = jnp.zeros_like(acc)
    low = lax.broadcasted_iota(jnp.int32, (LANES, LANES), 0).astype(bf16)
    low = jnp.concatenate([low] * (local // LANES), axis=1)
    one = jnp.ones((), bf16)
    zero = jnp.zeros((), bf16)
    group = math.gcd(owned, 32)

    def accumulate(step, carry):
        source = flipped(me, step, n)

        @pl.when(step > 0)
        def _():
            landed(recv_meta, meta_in, source)
            landed(recv_bins, bins_in, source)

        @pl.when(step == 1)
        def _():
            all_steps(start_stat)

        meta = recv_meta[source]
        hot = node == meta[2:3]
        weights = jnp.concatenate(
            [jnp.where(hot, meta[0:1], 0.0), jnp.where(hot, meta[1:2], 0.0)], axis=0
        ).astype(bf16)

        def some_features(block, carry):
            at = pl.ds(pl.multiple_of(block * group, group), group)
            row = recv_bins[source, at, :]
            highs = jnp.floor(row * (1.0 / LANES))
            rests = row - highs * LANES
            sums = []
            for j in range(group):
                rest = jnp.broadcast_to(rests[j : j + 1], (LANES, local)).astype(bf16)
                high = jnp.broadcast_to(highs[j : j + 1], weights.shape).astype(bf16)
                upto = jnp.where(rest <= low, one, zero)
                parts = [weights] + [
                    jnp.where(high == float(h), weights, zero) for h in range(1, HALVES)
                ]
                sums.append(
                    lax.dot_general(
                        jnp.concatenate(parts, axis=0), upto, (((1,), (1,)), ((), ())),
                        preferred_element_type=f32,
                    )
                )
            block_acc = acc.at[at]
            for j in range(group):
                block_acc[j] += sums[j]
            return carry

        return lax.fori_loop(0, owned // group, some_features, carry)

    def start_stat(step, carry):
        stat_copy(flipped(me, step, n)).start()
        return carry

    lax.fori_loop(0, n, accumulate, 0)

    def score(f, best):
        table = acc[f]
        upper = [table[2 * NODES * h : 2 * NODES * (h + 1)] for h in range(1, HALVES)]
        first = table[0 : 2 * NODES]
        for part in upper:
            first = first - part
        offset = jnp.zeros((2 * NODES, 1), f32)
        sums = []
        for part in [first] + upper:
            sums.append(part + offset)
            offset = offset + part[:, LANES - 1 : LANES]
        tot_grad, tot_hess = offset[:NODES], offset[NODES:]
        whole = tot_grad * tot_grad / (tot_hess + l2_penalty)
        for h, part in enumerate(sums):
            cum_grad, cum_hess = part[:NODES], part[NODES:]
            rest_grad = tot_grad - cum_grad
            gain = 0.5 * (
                cum_grad * cum_grad / (cum_hess + l2_penalty)
                + rest_grad * rest_grad / (tot_hess - cum_hess + l2_penalty)
                - whole
            )
            gains_ref[f, :, h * LANES : (h + 1) * LANES] = gain
            best = jnp.maximum(best, gain)
        return best

    best = lax.fori_loop(0, owned, score, jnp.full((NODES, LANES), -jnp.inf, f32))
    send_best[...] = to_row(jnp.max(best, axis=1, keepdims=True))
    recv_best[me] = send_best[...]

    def start_best(step, carry):
        best_copy(flipped(me, step, n)).start()
        return carry

    all_steps(start_best)

    def wait_stat(step, carry):
        landed(recv_stat, stat_in, flipped(me, step, n))
        return carry

    all_steps(wait_stat)
    stats = jnp.sum(recv_stat[...], axis=0)
    left_grad, left_hess = stats[0:1, :NODES], stats[0:1, NODES : 2 * NODES]
    node_grad, node_hess = stats[1:2, :NODES], stats[1:2, NODES : 2 * NODES]
    leaf_left = -left_grad / (left_hess + l2_penalty)
    leaf_right = -(node_grad - left_grad) / (node_hess - left_hess + l2_penalty)
    leaf_ref[0:1] = leaf_left
    leaf_ref[1:2] = leaf_right
    value = jnp.where(beyond, to_column(leaf_right), to_column(leaf_left))
    moved = jnp.sum(jnp.where(node_hot, value, 0.0), axis=0, keepdims=True)
    pred_ref[...] = old_ref[...] + shrinkage * moved

    def finish(step, carry):
        partner = flipped(me, step, n)
        meta_copy(partner).wait_send()
        bins_copy(partner).wait_send()
        stat_copy(partner).wait_send()
        best_copy(partner).wait_send()
        landed(recv_best, best_in, partner)
        return carry

    all_steps(finish)
    best_ref[...] = jnp.max(recv_best[...], axis=0)[:, :NODES]


def emit(gains_ref, best_ref, leaf_ref, pred_ref, gains_out, best_out, leaf_out, pred_out, sem):
    copy = pltpu.make_async_copy(gains_ref, gains_out, sem)
    copy.start()
    best_out[...] = best_ref[...]
    leaf_out[...] = leaf_ref[...]
    pred_out[...] = pred_ref[...]
    copy.wait()


def body(n, bin_ids, gradients, hessians, node_ids, predictions, split_feature, split_bin):
    assert n & (n - 1) == 0
    local, features = bin_ids.shape
    owned = features // n
    width = min(features, LANES)
    vmem = pl.BlockSpec(memory_space=pltpu.VMEM)
    hbm = pl.BlockSpec(memory_space=pltpu.HBM)
    shapes = (
        jax.ShapeDtypeStruct((owned, NODES, BINS), f32),
        jax.ShapeDtypeStruct((1, NODES), f32),
        jax.ShapeDtypeStruct((2, NODES), f32),
        jax.ShapeDtypeStruct((1, local), f32),
    )
    packed = (local // LANES, LANES)
    results = pl.pallas_call(
        functools.partial(kernel, n),
        out_shape=shapes,
        in_specs=[hbm] * 7,
        out_specs=(vmem,) * 4,
        scratch_shapes=[
            pltpu.VMEM((features // width, local, width), jnp.int32),
            pltpu.VMEM(packed, bf16),
            pltpu.VMEM(packed, bf16),
            pltpu.VMEM((1, local), jnp.int32),
            pltpu.VMEM((1, local), f32),
            pltpu.VMEM((1, NODES), jnp.int32),
            pltpu.VMEM((1, NODES), jnp.int32),
            pltpu.VMEM((n, owned, local), f32),
            pltpu.VMEM((3, local), f32),
            pltpu.VMEM((n, owned, local), f32),
            pltpu.VMEM((n, 3, local), f32),
            pltpu.VMEM((2, LANES), f32),
            pltpu.VMEM((n, 2, LANES), f32),
            pltpu.VMEM((1, LANES), f32),
            pltpu.VMEM((n, 1, LANES), f32),
            pltpu.VMEM((owned, 2 * NODES * HALVES, LANES), f32),
            pltpu.SemaphoreType.DMA((features // width,)),
            pltpu.SemaphoreType.DMA((6,)),
        ]
        + [pltpu.SemaphoreType.DMA((n,))] * 8,
        compiler_params=pltpu.CompilerParams(
            collective_id=0, has_side_effects=True, vmem_limit_bytes=48 << 20
        ),
        name="split_finding",
    )(
        bin_ids,
        gradients.reshape(packed),
        hessians.reshape(packed),
        node_ids.reshape(1, local),
        predictions.reshape(1, local),
        split_feature.reshape(1, NODES),
        split_bin.reshape(1, NODES),
    )
    gains, best, leaf, pred = pl.pallas_call(
        emit,
        out_shape=shapes,
        in_specs=[vmem] * 4,
        out_specs=(hbm, pl.BlockSpec(), pl.BlockSpec(), pl.BlockSpec()),
        scratch_shapes=[pltpu.SemaphoreType.DMA],
        name="emit",
    )(*results)
    return gains, best[0], leaf, pred[0]


def solution(mesh):
    both = P(("groups", "rows"))
    return jax.shard_map(
        functools.partial(body, mesh.shape["rows"]),
        mesh=mesh,
        in_specs=(
            P(("groups", "rows"), None), both, both, both, both, P("groups"), P("groups"),
        ),
        out_specs=(P(("groups", "rows"), None, None), P("groups"), P(None, "groups"), both),
        check_vma=False,
    )
```

```python
import functools
import math

import jax
import jax.numpy as jnp
from jax import lax
from jax.experimental import pallas as pl
from jax.experimental.pallas import tpu as pltpu
from jax.sharding import PartitionSpec as P

BINS = 256
NODES = 16
LANES = 128
HALVES = BINS // LANES

l2_penalty = 1.0
shrinkage = 0.5

f32 = jnp.float32
bf16 = jnp.bfloat16


def flipped(me, step, n):
    out, bit = 0, 1
    while bit < n:
        out = out + (((me // bit) % 2 + (step // bit) % 2) % 2) * bit
        bit *= 2
    return out


def to_row(column):
    shape = (column.shape[0], LANES)
    diagonal = lax.broadcasted_iota(jnp.int32, shape, 0) == lax.broadcasted_iota(
        jnp.int32, shape, 1
    )
    return jnp.sum(jnp.where(diagonal, column, 0.0), axis=0, keepdims=True)


def to_column(row):
    shape = (row.shape[1], row.shape[1])
    diagonal = lax.broadcasted_iota(jnp.int32, shape, 0) == lax.broadcasted_iota(
        jnp.int32, shape, 1
    )
    return jnp.sum(jnp.where(diagonal, row, 0.0), axis=1, keepdims=True)


def in_one_row(packed):
    pieces = [packed[j : j + 1].astype(f32) for j in range(packed.shape[0])]
    return jnp.concatenate(pieces, axis=1)


def kernel(
    n,
    bins_hbm,
    grad_hbm,
    hess_hbm,
    node_hbm,
    pred_hbm,
    feature_hbm,
    bin_hbm,
    gains_ref,
    best_ref,
    leaf_ref,
    pred_ref,
    bins_ref,
    grad_ref,
    hess_ref,
    node_ref,
    old_ref,
    feature_ref,
    bin_ref,
    send_bins,
    send_meta,
    recv_bins,
    recv_meta,
    send_stat,
    recv_stat,
    send_best,
    recv_best,
    acc,
    tile_sem,
    small_sem,
    bins_out,
    bins_in,
    meta_out,
    meta_in,
    stat_out,
    stat_in,
    best_out,
    best_in,
):
    owned = recv_bins.shape[1]
    local = recv_bins.shape[2]
    features = owned * n
    me = lax.axis_index("rows")
    width = bins_ref.shape[2]
    tiles = features // width
    per_tile = width // owned

    small = [
        pltpu.make_async_copy(source, target, small_sem.at[i])
        for i, (source, target) in enumerate(
            [
                (grad_hbm, grad_ref),
                (hess_hbm, hess_ref),
                (node_hbm, node_ref),
                (feature_hbm, feature_ref),
                (bin_hbm, bin_ref),
                (pred_hbm, old_ref),
            ]
        )
    ]
    for copy in small:
        copy.start()

    order = list(range(tiles))
    mine = me // per_tile
    tile_at = [flipped(mine, s, tiles) for s in order]
    loads = []
    for i, tile in enumerate(tile_at):
        columns = pl.ds(pl.multiple_of(tile * width, width), width)
        loads.append(
            pltpu.make_async_copy(bins_hbm.at[:, columns], bins_ref.at[i], tile_sem.at[i])
        )
        loads[-1].start()

    barrier = pltpu.get_barrier_semaphore()

    def all_steps(body):
        lax.fori_loop(1, n, body, 0)

    def greet(step, carry):
        pl.semaphore_signal(
            barrier, inc=1, device_id={"rows": flipped(me, step, n)},
            device_id_type=pl.DeviceIdType.MESH,
        )
        return carry

    all_steps(greet)

    def remote(to, source, target, out_sem, in_sem):
        return pltpu.make_async_remote_copy(
            src_ref=source, dst_ref=target.at[me],
            send_sem=out_sem.at[to], recv_sem=in_sem.at[me],
            device_id={"rows": to}, device_id_type=pl.DeviceIdType.MESH,
        )

    def bins_copy(to):
        return remote(to, send_bins.at[to], recv_bins, bins_out, bins_in)

    def meta_copy(to):
        return remote(to, send_meta, recv_meta, meta_out, meta_in)

    def stat_copy(to):
        return remote(to, send_stat, recv_stat, stat_out, stat_in)

    def best_copy(to):
        return remote(to, send_best, recv_best, best_out, best_in)

    def landed(buffer, sems, source):
        pltpu.make_async_copy(buffer.at[source], buffer.at[source], sems.at[source]).wait()

    for copy in small:
        copy.wait()
    send_meta[0:1] = in_one_row(grad_ref[...])
    send_meta[1:2] = in_one_row(hess_ref[...])
    send_meta[2:3] = node_ref[...].astype(f32)
    recv_meta[me] = send_meta[...]
    chosen = to_column(feature_ref[...].astype(f32))
    threshold = to_column(bin_ref[...].astype(f32))
    node = lax.broadcasted_iota(jnp.int32, (NODES, local), 0).astype(f32)
    node_hot = node == send_meta[2:3]

    pl.semaphore_wait(barrier, n - 1)

    def start_meta(step, carry):
        meta_copy(flipped(me, step, n)).start()
        return carry

    def send_tile(tile):
        def start(j, carry):
            to = tile * per_tile + flipped(me % per_tile, j, per_tile)

            @pl.when(to != me)
            def _():
                bins_copy(to).start()

            return carry

        lax.fori_loop(0, per_tile, start, 0)

    node_bin = jnp.zeros((NODES, local), f32)
    for i, tile in enumerate(tile_at):
        loads[i].wait()
        turned = jnp.transpose(bins_ref[i].astype(f32))
        for j in range(per_tile):
            send_bins[tile * per_tile + j] = turned[j * owned : (j + 1) * owned]
        if i == 0:
            all_steps(start_meta)
        else:
            send_tile(tile_at[i - 1])
        feature = lax.broadcasted_iota(jnp.int32, (NODES, width), 1) + tile * width
        pick = jnp.where(feature.astype(f32) == chosen, 1.0, 0.0).astype(bf16)
        node_bin = node_bin + jnp.dot(
            pick, turned.astype(bf16), preferred_element_type=f32
        )
    send_tile(tile_at[-1])
    recv_bins[me] = send_bins[me]

    beyond = node_bin > threshold
    for i, hot in enumerate((node_hot & jnp.logical_not(beyond), node_hot)):
        exact = jnp.concatenate(
            [jnp.where(hot, send_meta[0:1], 0.0), jnp.where(hot, send_meta[1:2], 0.0)], axis=0
        )
        send_stat[i : i + 1] = to_row(jnp.sum(exact, axis=1, keepdims=True))
    recv_stat[me] = send_stat[...]

    acc[...] = jnp.zeros_like(acc)
    low = lax.broadcasted_iota(jnp.int32, (LANES, LANES), 0).astype(bf16)
    low = jnp.concatenate([low] * (local // LANES), axis=1)
    one = jnp.ones((), bf16)
    zero = jnp.zeros((), bf16)
    group = math.gcd(owned, 32)

    def accumulate(step, carry):
        source = flipped(me, step, n)

        @pl.when(step > 0)
        def _():
            landed(recv_meta, meta_in, source)
            landed(recv_bins, bins_in, source)

        @pl.when(step == 1)
        def _():
            all_steps(start_stat)

        meta = recv_meta[source]
        hot = node == meta[2:3]
        weights = jnp.concatenate(
            [jnp.where(hot, meta[0:1], 0.0), jnp.where(hot, meta[1:2], 0.0)], axis=0
        ).astype(bf16)

        def some_features(block, carry):
            at = pl.ds(pl.multiple_of(block * group, group), group)
            row = recv_bins[source, at, :]
            highs = jnp.floor(row * (1.0 / LANES))
            rests = row - highs * LANES
            sums = []
            for j in range(group):
                rest = jnp.broadcast_to(rests[j : j + 1], (LANES, local)).astype(bf16)
                high = jnp.broadcast_to(highs[j : j + 1], weights.shape).astype(bf16)
                upto = jnp.where(rest <= low, one, zero)
                parts = [weights] + [
                    jnp.where(high == float(h), weights, zero) for h in range(1, HALVES)
                ]
                sums.append(
                    lax.dot_general(
                        jnp.concatenate(parts, axis=0), upto, (((1,), (1,)), ((), ())),
                        preferred_element_type=f32,
                    )
                )
            block_acc = acc.at[at]
            for j in range(group):
                block_acc[j] += sums[j]
            return carry

        return lax.fori_loop(0, owned // group, some_features, carry)

    def start_stat(step, carry):
        stat_copy(flipped(me, step, n)).start()
        return carry

    lax.fori_loop(0, n, accumulate, 0)

    def score(f, best):
        table = acc[f]
        upper = [table[2 * NODES * h : 2 * NODES * (h + 1)] for h in range(1, HALVES)]
        first = table[0 : 2 * NODES]
        for part in upper:
            first = first - part
        offset = jnp.zeros((2 * NODES, 1), f32)
        sums = []
        for part in [first] + upper:
            sums.append(part + offset)
            offset = offset + part[:, LANES - 1 : LANES]
        tot_grad, tot_hess = offset[:NODES], offset[NODES:]
        whole = tot_grad * tot_grad / (tot_hess + l2_penalty)
        for h, part in enumerate(sums):
            cum_grad, cum_hess = part[:NODES], part[NODES:]
            rest_grad = tot_grad - cum_grad
            gain = 0.5 * (
                cum_grad * cum_grad / (cum_hess + l2_penalty)
                + rest_grad * rest_grad / (tot_hess - cum_hess + l2_penalty)
                - whole
            )
            gains_ref[f, :, h * LANES : (h + 1) * LANES] = gain
            best = jnp.maximum(best, gain)
        return best

    best = lax.fori_loop(0, owned, score, jnp.full((NODES, LANES), -jnp.inf, f32))
    send_best[...] = to_row(jnp.max(best, axis=1, keepdims=True))
    recv_best[me] = send_best[...]

    def start_best(step, carry):
        best_copy(flipped(me, step, n)).start()
        return carry

    all_steps(start_best)

    def wait_stat(step, carry):
        landed(recv_stat, stat_in, flipped(me, step, n))
        return carry

    all_steps(wait_stat)
    stats = jnp.sum(recv_stat[...], axis=0)
    left_grad, left_hess = stats[0:1, :NODES], stats[0:1, NODES : 2 * NODES]
    node_grad, node_hess = stats[1:2, :NODES], stats[1:2, NODES : 2 * NODES]
    leaf_left = -left_grad / (left_hess + l2_penalty)
    leaf_right = -(node_grad - left_grad) / (node_hess - left_hess + l2_penalty)
    leaf_ref[0:1] = leaf_left
    leaf_ref[1:2] = leaf_right
    value = jnp.where(beyond, to_column(leaf_right), to_column(leaf_left))
    moved = jnp.sum(jnp.where(node_hot, value, 0.0), axis=0, keepdims=True)
    pred_ref[...] = old_ref[...] + shrinkage * moved

    def finish(step, carry):
        partner = flipped(me, step, n)
        meta_copy(partner).wait_send()
        bins_copy(partner).wait_send()
        stat_copy(partner).wait_send()
        best_copy(partner).wait_send()
        landed(recv_best, best_in, partner)
        return carry

    all_steps(finish)
    best_ref[...] = jnp.max(recv_best[...], axis=0)[:, :NODES]


def body(n, bin_ids, gradients, hessians, node_ids, predictions, split_feature, split_bin):
    assert n & (n - 1) == 0
    local, features = bin_ids.shape
    owned = features // n
    width = min(features, LANES)
    vmem = pl.BlockSpec(memory_space=pltpu.VMEM)
    hbm = pl.BlockSpec(memory_space=pltpu.HBM)
    shapes = (
        jax.ShapeDtypeStruct((owned, NODES, BINS), f32),
        jax.ShapeDtypeStruct((1, NODES), f32),
        jax.ShapeDtypeStruct((2, NODES), f32),
        jax.ShapeDtypeStruct((1, local), f32),
    )
    packed = (local // LANES, LANES)
    results = pl.pallas_call(
        functools.partial(kernel, n),
        out_shape=shapes,
        in_specs=[hbm] * 7,
        out_specs=(vmem,) * 4,
        scratch_shapes=[
            pltpu.VMEM((features // width, local, width), jnp.int32),
            pltpu.VMEM(packed, bf16),
            pltpu.VMEM(packed, bf16),
            pltpu.VMEM((1, local), jnp.int32),
            pltpu.VMEM((1, local), f32),
            pltpu.VMEM((1, NODES), jnp.int32),
            pltpu.VMEM((1, NODES), jnp.int32),
            pltpu.VMEM((n, owned, local), f32),
            pltpu.VMEM((3, local), f32),
            pltpu.VMEM((n, owned, local), f32),
            pltpu.VMEM((n, 3, local), f32),
            pltpu.VMEM((2, LANES), f32),
            pltpu.VMEM((n, 2, LANES), f32),
            pltpu.VMEM((1, LANES), f32),
            pltpu.VMEM((n, 1, LANES), f32),
            pltpu.VMEM((owned, 2 * NODES * HALVES, LANES), f32),
            pltpu.SemaphoreType.DMA((features // width,)),
            pltpu.SemaphoreType.DMA((6,)),
        ]
        + [pltpu.SemaphoreType.DMA((n,))] * 8,
        compiler_params=pltpu.CompilerParams(
            collective_id=0, has_side_effects=True, vmem_limit_bytes=60 * 1024 * 1024
        ),
        name="split_finding",
    )(
        bin_ids,
        gradients.reshape(packed),
        hessians.reshape(packed),
        node_ids.reshape(1, local),
        predictions.reshape(1, local),
        split_feature.reshape(1, NODES),
        split_bin.reshape(1, NODES),
    )
    gains, best, leaf, pred = results
    return gains, best[0], leaf, pred[0]


def solution(mesh):
    both = P(("groups", "rows"))
    return jax.shard_map(
        functools.partial(body, mesh.shape["rows"]),
        mesh=mesh,
        in_specs=(
            P(("groups", "rows"), None), both, both, both, both, P("groups"), P("groups"),
        ),
        out_specs=(P(("groups", "rows"), None, None), P("groups"), P(None, "groups"), both),
        check_vma=False,
    )
```
